32 devices in a mesh: slab: 8 (over z, core), loop: 4 (over y, x).
Axes of the slice: x: 2, y: 2, z: 4, core: 2. Of those that a mesh axis runs over, the one named last changes fastest.
Arguments:
- doc_pool: bfloat16 [8, 4, 256, 4096], P('slab', 'loop'), may hold values from -6 to 6
- cand_owner: int32 [8, 4, 16, 1], P('slab', 'loop'), may hold values from 0 to 7; in each aligned block of 16 rows (0 to 15, 16 to 31, ..., all dimensions but the last counted through in order) at most 4 rows name the same one
- cand_row: int32 [8, 4, 16], P('slab', 'loop'), may hold values from 0 to 255
- elements: bfloat16 [8, 4, 2048, 4096], P('slab', 'loop'), may hold values from -6 to 6
- coverage: float32 [8, 4, 2048], P('slab', 'loop'), may hold values from -0.5 to 1.5
- elem_weight: float32 [8, 4, 2048], P('slab', 'loop'), may hold values from 1 to 10
Outputs:
- gains: float32 [8, 4, 16], P('slab', 'loop')
The draws below stay inside these ranges and needn't reach their ends.
Inputs may be any that keep to these rules, and one draw needn't show every extreme that they name: `cand_owner`: among the candidates of one device, at most 4 name the same owner; some owner is named exactly 4 times.
All inputs are finite; a program needn't handle non-finite values.
Results may differ from the reference program's by a relative error of at most 0.0003.
Values may be sent and summed in bfloat16 or wider, within the bound.
A program may use at most 128 MiB of HBM per device.

```python
import math
import jax
import jax.numpy as jnp
import numpy as np
from jax import lax

D = 4096
CB = 128
ELEM_DEV = 2048
POOL_DEV = 256
CAP = 4
ELEMS = 65536
N_SLAB = 8
N_LOOP = 4


def plant(drawn, key, least, largest):
    extent = drawn.shape
    index_at = [jax.random.randint(jax.random.fold_in(key, axis), (), 0, extent[axis]) for axis in range(len(extent))]
    drawn = drawn.at[tuple(index_at)].set(least)
    longest = extent.index(max(extent))
    index_at[longest] = (index_at[longest] + 1) % extent[longest]
    return drawn.at[tuple(index_at)].set(largest)


def level_of(rng, extent, cuts, smallest, top_value):
    def one(axis_at, parts):
        heights = jax.random.uniform(jax.random.fold_in(jax.random.fold_in(rng, 6), axis_at), (parts,), jnp.float32, smallest / len(cuts), top_value / len(cuts))
        return jnp.repeat(jnp.exp(heights), extent[axis_at] // parts).reshape((-1,) + (1,) * (len(extent) - axis_at - 1))

    factor_of = one(*cuts[0])
    for cut in cuts[1:]:
        factor_of = factor_of * one(*cut)
    return factor_of


def deal_out(key, own, number, rows, count, top, most, skew):
    ranking = jax.random.permutation(key, count)
    packed, common = portions_of(count, rows * top, most, skew, True), portions_of(count, rows * top, most, skew, False)
    places = jnp.arange(count)

    def named(lengths, rotation):
        used = int((lengths > 0).sum())
        fixed = max(1, used // 4)
        shifted = fixed + (places - fixed + rotation * (used - fixed)) % max(1, count - fixed)
        return jnp.zeros((count,), jnp.int32).at[ranking[jnp.where(places < fixed, places, shifted)]].set(jnp.asarray(lengths, jnp.int32))

    lengths = jnp.where(number % 4 == 0, named(packed, number // 4), named(common, number - number // 4 - 1))
    mixed = jax.random.permutation(jax.random.fold_in(own, 3), count)
    source_of, taker = mixed[0:count // 2 * 2:2], mixed[1:count // 2 * 2:2]
    margin = jnp.minimum(lengths[source_of] - 1, most - lengths[taker]) // 2
    margin = jnp.where((source_of == ranking[0]) | (taker == ranking[0]) | (lengths[taker] == 0), 0, jnp.maximum(margin, 0))
    shifted = jax.random.randint(jax.random.fold_in(own, 4), (count // 2,), 0, 1 << 20) % (margin + 1)
    lengths = lengths.at[source_of].add(-shifted).at[taker].add(shifted)
    labels = jnp.searchsorted(jnp.cumsum(lengths), jnp.arange(rows * top), side="right").astype(jnp.int32)
    table = labels.reshape(top, rows).T
    table = table[jax.random.permutation(jax.random.fold_in(own, 1), rows)]
    rotation = jax.random.randint(jax.random.fold_in(own, 2), (rows, 1), 0, top)
    return jnp.take_along_axis(table, (jnp.arange(top)[None, :] + rotation) % top, axis=1)


def portions_of(amount, total, bound, lean, full):
    weights = [(1 << 20) // math.isqrt(standing ** lean) + 1 for standing in range(1, amount + 1)]
    largest = bound if full else min(bound, max(-(-total // amount), total * weights[0] // sum(weights)))
    least = 1 if total - largest >= amount - 1 else 0
    holding, rest = [largest] + [least] * (amount - 1), total - largest - least * (amount - 1)
    while rest > 0:
        candidates = [i for i in range(1, amount) if holding[i] < largest] or [i for i in range(1, amount) if holding[i] < bound]
        pool, budget = sum([weights[i] for i in candidates]), rest
        for i in candidates:
            extra = min(bound - holding[i], max(1, budget * weights[i] // pool), rest)
            holding[i] = holding[i] + extra
            rest = rest - extra
    return np.array(holding)


def centred(stream_key, extent, width, bound, pieces=(), kind=jnp.bfloat16):
    gain = level_of(stream_key, extent, pieces, -0.22, 0.18) if pieces else 1.0
    values = jax.random.normal(stream_key, extent, jnp.float32) * width * gain
    return jnp.minimum(jnp.maximum(values, -bound), bound).astype(kind)


def setup_inputs(seed: int = 0) -> dict:
    key_of = jax.random.split(jax.random.key(seed), 7)
    doc_pool = centred(key_of[0], (N_SLAB, N_LOOP, POOL_DEV, D), 1.0, 6.0, ((0, 8), (1, 4)))
    cand_owner_keys = jax.random.split(jax.random.fold_in(key_of[1], 1), N_SLAB * N_LOOP * (CB // N_SLAB) // (CB // N_SLAB))
    cand_owner_turns = jax.random.permutation(jax.random.fold_in(key_of[1], 3), N_SLAB * N_LOOP * (CB // N_SLAB) // (CB // N_SLAB))
    cand_owner = jax.vmap(lambda own, number: deal_out(jax.random.fold_in(key_of[1], 2), own, number, CB // N_SLAB, N_SLAB, 1, CAP, 2))(cand_owner_keys, cand_owner_turns).reshape((N_SLAB, N_LOOP, CB // N_SLAB, 1))
    cand_row = plant(jax.random.randint(key_of[2], (N_SLAB, N_LOOP, CB // N_SLAB), 0, POOL_DEV), jax.random.fold_in(key_of[2], 1), 0, POOL_DEV - 1).astype(jnp.int32)
    elements = centred(key_of[3], (N_SLAB, N_LOOP, ELEM_DEV, D), 1.0, 6.0, ((0, 8), (1, 4)))
    coverage = jnp.clip(-0.5 + 2.0 * jax.random.uniform(key_of[4], (N_SLAB, N_LOOP, ELEM_DEV), jnp.float32) ** level_of(key_of[4], (N_SLAB, N_LOOP, ELEM_DEV), ((0, 8), (1, 4)), -0.2, 0.2), -0.5, 1.5)
    elem_weight = jnp.clip(jnp.exp(math.log(10.0) - 2.3025851 * jax.random.uniform(key_of[5], (N_SLAB, N_LOOP, ELEM_DEV), jnp.float32) ** level_of(key_of[5], (N_SLAB, N_LOOP, ELEM_DEV), ((0, 8), (1, 4)), -0.2, 0.2)), 1.0, 10.0)
    return dict(doc_pool=doc_pool, cand_owner=cand_owner, cand_row=cand_row, elements=elements, coverage=coverage, elem_weight=elem_weight)


def reference(doc_pool, cand_owner, cand_row, elements, coverage, elem_weight):
    owner_ids = cand_owner[..., 0]
    column_ids = jnp.broadcast_to(jnp.arange(N_LOOP, dtype=jnp.int32)[None, :, None], owner_ids.shape)
    cand_emb = doc_pool[owner_ids, column_ids, cand_row]
    cand_flat = cand_emb.reshape(-1, D)
    sim_scale = float(D) ** -0.5
    shard_elems = elements.reshape(N_SLAB * N_LOOP, ELEM_DEV, D)
    shard_cover = coverage.reshape(N_SLAB * N_LOOP, ELEM_DEV)
    shard_weight = elem_weight.reshape(N_SLAB * N_LOOP, ELEM_DEV)

    def accumulate(running, shard):
        docs, cover_part, weight_part = shard
        scores = jnp.dot(docs, cand_flat.T, preferred_element_type=jnp.float32) * sim_scale
        term = jnp.sum(weight_part[:, None] * jnp.maximum(scores - cover_part[:, None], 0.0), axis=0)
        return running + term, None

    init = jnp.zeros((cand_flat.shape[0],), jnp.float32)
    running, _ = lax.scan(accumulate, init, (shard_elems, shard_cover, shard_weight))
    gains = running / float(ELEMS)
    return gains.reshape(owner_ids.shape)
```

```python
import functools

import jax
import jax.numpy as jnp
from jax import lax
from jax.experimental import pallas as pl
from jax.experimental.pallas import tpu as pltpu
from jax.sharding import PartitionSpec as P

MESH = pl.DeviceIdType.MESH
LANES = 128
SUB = 8


def kernel(
    dims,
    owner_ref, row_ref, cover_ref, weight_ref, pool_hbm, docs_hbm,
    out_ref,
    pool, docs, req_out, req_in, picked, fetched, cand, acc, part, terms,
    pool_sem, docs_sem, req_send, req_recv, pick_send, pick_recv, self_sem,
    unit_send, unit_recv, term_send, term_recv,
):
    slabs, loops, share, cap, chunks, chunk, tile, total_docs, scale = dims
    lines = slabs // 2
    units = slabs * loops
    rows_pool = pool.shape[0]
    n_docs = docs.shape[1]
    slab = lax.axis_index("slab")
    loop = lax.axis_index("loop")
    line = slab // 2
    core = lax.rem(slab, 2)
    me = slab * loops + loop
    half = loops // 2

    def loop_of(pos):
        return jnp.where(pos < half, 2 * pos, 2 * (loops - 1 - pos) + 1)

    here = jnp.where(lax.rem(loop, 2) == 0, loop // 2, loops - 1 - loop // 2)
    ahead = loop_of(lax.rem(here + 1, loops))
    behind = loop_of(lax.rem(here + loops - 1, loops))

    pool_copy = [
        pltpu.make_async_copy(
            pool_hbm.at[:, pl.ds(k * chunk, chunk)],
            pool.at[:, pl.ds(k * chunk, chunk)],
            pool_sem.at[k],
        )
        for k in range(chunks)
    ]
    docs_copy = [
        pltpu.make_async_copy(
            docs_hbm.at[:, pl.ds(k * chunk, chunk)], docs.at[k], docs_sem.at[k]
        )
        for k in range(chunks)
    ]

    barrier = pltpu.get_barrier_semaphore()

    def greet(d, _):
        other = lax.rem(me + d, units)
        pl.semaphore_signal(
            barrier, inc=1, device_id=(other // loops, lax.rem(other, loops)), device_id_type=MESH
        )
        return 0

    lax.fori_loop(1, units, greet, 0)
    for k in range(chunks):
        pool_copy[k].start()
    for k in range(chunks):
        docs_copy[k].start()

    owner_row = owner_ref[...]
    row_row = row_ref[...]
    down = lax.broadcasted_iota(jnp.int32, (share, share), 0)
    across = lax.broadcasted_iota(jnp.int32, (share, share), 1)
    wide = jnp.broadcast_to(owner_row, (share, share)).astype(jnp.float32)
    owner_col = jnp.sum(jnp.where(down == across, wide, 0.0), axis=1, keepdims=True)
    rank_row = jnp.sum(
        jnp.where((owner_col == wide) & (down < across), 1.0, 0.0), axis=0, keepdims=True
    )
    owner_f = owner_row.astype(jnp.float32)
    asked_row = owner_f * SUB + rank_row
    slot_row = owner_f * cap + rank_row
    slot_col = jnp.sum(
        jnp.where(down == across, jnp.broadcast_to(slot_row, (share, share)), 0.0),
        axis=1, keepdims=True,
    )
    place = lax.broadcasted_iota(jnp.int32, (slabs * SUB, share), 0).astype(jnp.float32)
    asked = jnp.sum(
        jnp.where(place == asked_row, row_row.astype(jnp.float32), 0.0), axis=1, keepdims=True
    )
    req_out[...] = jnp.broadcast_to(asked, (slabs * SUB, LANES)).astype(jnp.int32).reshape(
        slabs, SUB, LANES
    )
    choose = jnp.where(
        slot_col == lax.broadcasted_iota(jnp.int32, (share, slabs * cap), 1).astype(jnp.float32),
        1.0, 0.0,
    ).astype(jnp.bfloat16)

    pl.semaphore_wait(barrier, units - 1)

    def req_copy(d):
        other = lax.rem(slab + d, slabs)
        return pltpu.make_async_remote_copy(
            src_ref=req_out.at[other], dst_ref=req_in.at[slab],
            send_sem=req_send.at[d], recv_sem=req_recv.at[d],
            device_id=(other, loop), device_id_type=MESH,
        )

    for d in range(1, slabs):
        req_copy(d).start()
    own_req = pltpu.make_async_copy(req_out.at[slab], req_in.at[slab], self_sem.at[chunks])
    own_req.start()
    own_req.wait()
    for d in range(1, slabs):
        req_copy(d).wait()

    wanted = req_in[...].reshape(slabs * SUB, LANES)
    lane = lax.broadcasted_iota(jnp.int32, (slabs * SUB, LANES), 1)
    pick = jnp.concatenate(
        [
            jnp.where(wanted == lane + b * LANES, 1.0, 0.0).astype(jnp.bfloat16)
            for b in range(rows_pool // LANES)
        ],
        axis=1,
    )

    def pick_copy(k, d):
        other = lax.rem(slab + d, slabs)
        return pltpu.make_async_remote_copy(
            src_ref=picked.at[k, other], dst_ref=fetched.at[k, slab],
            send_sem=pick_send.at[k, d], recv_sem=pick_recv.at[k, d],
            device_id=(other, loop), device_id_type=MESH,
        )

    def own_pick(k):
        return pltpu.make_async_copy(picked.at[k, slab], fetched.at[k, slab], self_sem.at[k])

    def gather(k):
        pool_copy[k].wait()
        rows = jnp.dot(
            pick, pool[:, k * chunk:(k + 1) * chunk], preferred_element_type=jnp.float32
        )
        for r in range(slabs):
            picked[k, r] = rows[r * SUB:r * SUB + cap].astype(jnp.bfloat16)
        for d in range(1, slabs):
            pick_copy(k, d).start()
        own_pick(k).start()

    def unit_of(j, pos, c):
        return (2 * j + c) * loops + loop_of(pos)

    def unit_copy(k, j, pos, way):
        u = unit_of(j, pos, core)
        if way == 0:
            device = (2 * jnp.minimum(line + 1, lines - 1) + core, loop)
        elif way == 1:
            device = (2 * jnp.maximum(line - 1, 0) + core, loop)
        elif way == 2:
            device = (slab, ahead)
        elif way == 3:
            device = (slab, behind)
        else:
            device = (2 * line + 1 - core, loop)
        return pltpu.make_async_remote_copy(
            src_ref=cand.at[k, u], dst_ref=cand.at[k, u],
            send_sem=unit_send.at[k, j * loops + pos, way], recv_sem=unit_recv.at[k, u],
            device_id=device, device_id_type=MESH,
        )

    def arrive(k, j, pos, c):
        u = unit_of(j, pos, c)
        pltpu.make_async_remote_copy(
            src_ref=cand.at[k, u], dst_ref=cand.at[k, u],
            send_sem=unit_send.at[k, 0, 0], recv_sem=unit_recv.at[k, u],
            device_id=(2 * line + 1 - core, loop), device_id_type=MESH,
        ).wait_recv()

    reach_even, reach_odd = half, loops - 1 - half

    def forward(k, j, pos, finish=False):
        def act(cond, way):
            @pl.when(cond)
            def _():
                copy = unit_copy(k, j, pos, way)
                if finish:
                    copy.wait_send()
                else:
                    copy.start()
        from_here = pos == here
        far_ahead = lax.rem(here - pos + loops, loops)
        far_behind = lax.rem(pos - here + loops, loops)
        reach_ahead = jnp.where(core == 0, reach_even, reach_odd)
        reach_behind = jnp.where(core == 0, reach_odd, reach_even)
        by_ahead = far_ahead <= reach_ahead
        act(from_here & (j <= line) & (line + 1 < lines), 0)
        act(from_here & (j >= line) & (line > 0), 1)
        act(from_here | (by_ahead & (far_ahead < reach_ahead)), 2)
        act(from_here | (jnp.logical_not(by_ahead) & (far_behind < reach_behind)), 3)
        act(from_here | True, 4)

    def nearby(first, action):
        def step(t, _):
            far = (t + 1) // 2
            j = jnp.where(lax.rem(t, 2) == 1, line - far, line + far)

            @pl.when((j >= 0) & (j < lines))
            def _():
                action(j)
            return 0
        lax.fori_loop(first, 2 * lines - 1, step, 0)

    def own(k):
        own_pick(k).wait()
        for d in range(1, slabs):
            pick_copy(k, d).wait()
        rows = jnp.concatenate(
            [fetched[k, o].astype(jnp.float32) for o in range(slabs)], axis=0
        ).astype(jnp.bfloat16)
        mine = jnp.dot(choose, rows, preferred_element_type=jnp.float32)
        cand[k, me] = mine.astype(jnp.bfloat16)
        forward(k, line, here)

    def column(k):
        def action(j):
            arrive(k, j, here, core)
            forward(k, j, here)
        nearby(1, action)

    def ring(k, e):
        def action(j):
            behind_pos = lax.rem(here - e + loops, loops)
            ahead_pos = lax.rem(here + e, loops)
            reach_ahead = jnp.where(core == 0, reach_even, reach_odd)
            reach_behind = jnp.where(core == 0, reach_odd, reach_even)

            @pl.when(e <= reach_ahead)
            def _():
                arrive(k, j, behind_pos, core)
                forward(k, j, behind_pos)

            @pl.when(e <= reach_behind)
            def _():
                arrive(k, j, ahead_pos, core)
                forward(k, j, ahead_pos)
        nearby(0, action)

    def sibling(k):
        def step(t, _):
            arrive(k, t // loops, lax.rem(t, loops), 1 - core)
            return 0
        lax.fori_loop(0, lines * loops, step, 0)

    def multiply(k):
        docs_copy[k].wait()
        share_all = cand[k].reshape(units * share, chunk)

        def step(i, _):
            at = pl.ds(pl.multiple_of(i * tile, tile), tile)
            product = lax.dot_general(
                docs[k, at, :], share_all, (((1,), (1,)), ((), ())),
                preferred_element_type=jnp.float32,
            )
            if k == 0:
                acc[at, :] = product
            else:
                acc[at, :] += product
            return 0
        lax.fori_loop(0, n_docs // tile, step, 0)

    for k in range(min(2, chunks)):
        gather(k)
    own(0)
    column(0)
    for k in range(chunks):
        if k + 2 < chunks:
            gather(k + 2)
        ring(k, 1)
        if k + 1 < chunks:
            own(k + 1)
            column(k + 1)
        for e in range(2, half + 1):
            ring(k, e)
        if k > 0:
            sibling(k - 1)
            multiply(k - 1)
    sibling(chunks - 1)
    multiply(chunks - 1)

    cover_cols = jnp.transpose(cover_ref[...])
    weight_cols = jnp.transpose(weight_ref[...])
    total = jnp.zeros((1, units * share), jnp.float32)
    for j in range(n_docs // LANES):
        s = acc[j * LANES:(j + 1) * LANES, :] * scale
        gain = weight_cols[:, j:j + 1] * jnp.maximum(s - cover_cols[:, j:j + 1], 0.0)
        total = total + jnp.sum(gain, axis=0, keepdims=True)
    total = total / total_docs
    per_row = LANES // share
    for r in range(units // per_row):
        part[r] = total[:, r * LANES:(r + 1) * LANES]

    def term_copy(d):
        other = lax.rem(me + d, units)
        return pltpu.make_async_remote_copy(
            src_ref=part.at[other // per_row], dst_ref=terms.at[d],
            send_sem=term_send.at[d], recv_sem=term_recv.at[d],
            device_id=(other // loops, lax.rem(other, loops)), device_id_type=MESH,
        )

    def send_term(d, _):
        term_copy(d).start()
        return 0

    def take_term(d, _):
        term_copy(d).wait()
        return 0

    lax.fori_loop(1, units, send_term, 0)
    terms[0] = part[me // per_row]
    for k in range(chunks):
        def finish(t, _, k=k):
            forward(k, t // loops, lax.rem(t, loops), finish=True)
            return 0
        lax.fori_loop(0, lines * loops, finish, 0)
    lax.fori_loop(1, units, take_term, 0)
    out_ref[...] = jnp.sum(terms[...], axis=0)


def body(dims, doc_pool, cand_owner, cand_row, elements, coverage, elem_weight):
    slabs, loops, share, cap, chunks, chunk, tile, _, _ = dims
    pool_rows, width = doc_pool.shape[2:]
    n_docs = elements.shape[2]
    units = slabs * loops
    per_row = LANES // share
    vmem = pl.BlockSpec(memory_space=pltpu.VMEM)
    hbm = pl.BlockSpec(memory_space=pl.ANY)
    dma = pltpu.SemaphoreType.DMA
    out = pl.pallas_call(
        functools.partial(kernel, dims),
        out_shape=jax.ShapeDtypeStruct((1, LANES), jnp.float32),
        in_specs=[vmem, vmem, vmem, vmem, hbm, hbm],
        out_specs=vmem,
        scratch_shapes=[
            pltpu.VMEM((pool_rows, width), jnp.bfloat16),
            pltpu.VMEM((chunks, n_docs, chunk), jnp.bfloat16),
            pltpu.VMEM((slabs, SUB, LANES), jnp.int32),
            pltpu.VMEM((slabs, SUB, LANES), jnp.int32),
            pltpu.VMEM((chunks, slabs, cap, chunk), jnp.bfloat16),
            pltpu.VMEM((chunks, slabs, cap, chunk), jnp.bfloat16),
            pltpu.VMEM((chunks, units, share, chunk), jnp.bfloat16),
            pltpu.VMEM((n_docs, units * share), jnp.float32),
            pltpu.VMEM((units // per_row, 1, LANES), jnp.float32),
            pltpu.VMEM((units, 1, LANES), jnp.float32),
            dma((chunks,)),
            dma((chunks,)),
            dma((slabs,)),
            dma((slabs,)),
            dma((chunks, slabs)),
            dma((chunks, slabs)),
            dma((chunks + 1,)),
            dma((chunks, units // 2, 5)),
            dma((chunks, units)),
            dma((units,)),
            dma((units,)),
        ],
        compiler_params=pltpu.CompilerParams(
            collective_id=0, has_side_effects=True, vmem_limit_bytes=60 * 2**20
        ),
    )(
        cand_owner.reshape(1, share),
        cand_row.reshape(1, share),
        coverage.reshape(n_docs // LANES, LANES),
        elem_weight.reshape(n_docs // LANES, LANES),
        doc_pool.reshape(pool_rows, width),
        elements.reshape(n_docs, width),
    )
    me = lax.axis_index("slab") * loops + lax.axis_index("loop")
    mine = lax.dynamic_slice(out, (0, lax.rem(me, per_row) * share), (1, share))
    return mine.reshape(1, 1, share)


def solution(mesh):
    slabs, loops = mesh.shape["slab"], mesh.shape["loop"]

    def whole(doc_pool, cand_owner, cand_row, elements, coverage, elem_weight):
        share = cand_row.shape[2]
        width = doc_pool.shape[3]
        n_docs = elements.shape[2]
        cap = max(2, 2 * share // slabs)
        chunks = 4
        dims = (
            slabs, loops, share, cap, chunks, width // chunks, min(512, n_docs),
            float(n_docs * slabs * loops), float(width) ** (-0.5),
        )
        placed = (
            P("slab", "loop", None, None),
            P("slab", "loop", None, None),
            P("slab", "loop", None),
            P("slab", "loop", None, None),
            P("slab", "loop", None),
            P("slab", "loop", None),
        )
        return jax.shard_map(
            functools.partial(body, dims), mesh=mesh, in_specs=placed,
            out_specs=P("slab", "loop", None), check_vma=False,
        )(doc_pool, cand_owner, cand_row, elements, coverage, elem_weight)

    return whole
```

```python
import functools

import jax
import jax.numpy as jnp
from jax import lax
from jax.experimental import pallas as pl
from jax.experimental.pallas import tpu as pltpu
from jax.sharding import PartitionSpec as P

MESH = pl.DeviceIdType.MESH
LANES = 128
SUB = 8


def kernel(
    dims,
    owner_ref, row_ref, cover_ref, weight_ref, pool_hbm, docs_hbm,
    out_ref,
    pool, docs, req_out, req_in, picked, fetched, cand, acc, part, slab_terms,
    loop_terms,
    pool_sem, docs_sem, req_send, req_recv, pick_send, pick_recv, self_sem,
    unit_send, line_send, unit_recv, slab_send, slab_recv, loop_send, loop_recv,
):
    slabs, loops, share, cap, chunks, chunk, tile, total_docs, scale = dims
    lines = slabs // 2
    units = slabs * loops
    rows_pool = pool.shape[0]
    n_docs = docs.shape[1]
    slab = lax.axis_index("slab")
    loop = lax.axis_index("loop")
    line = slab // 2
    core = lax.rem(slab, 2)
    me = slab * loops + loop
    half = loops // 2
    pieces = 2

    def loop_of(pos):
        return jnp.where(pos < half, 2 * pos, 2 * (loops - 1 - pos) + 1)

    here = jnp.where(lax.rem(loop, 2) == 0, loop // 2, loops - 1 - loop // 2)
    ahead = loop_of(lax.rem(here + 1, loops))
    behind = loop_of(lax.rem(here + loops - 1, loops))

    pool_copy = [
        pltpu.make_async_copy(
            pool_hbm.at[:, pl.ds(k * chunk, chunk)],
            pool.at[:, pl.ds(k * chunk, chunk)],
            pool_sem.at[k],
        )
        for k in range(chunks)
    ]
    docs_copy = [
        pltpu.make_async_copy(
            docs_hbm.at[:, pl.ds(k * chunk, chunk)], docs.at[k], docs_sem.at[k]
        )
        for k in range(chunks)
    ]

    barrier = pltpu.get_barrier_semaphore()

    def greet(device):
        pl.semaphore_signal(barrier, inc=1, device_id=device, device_id_type=MESH)

    for d in range(1, slabs):
        greet((lax.rem(slab + d, slabs), loop))
    for d in range(1, loops):
        greet((slab, lax.rem(loop + d, loops)))
    for k in range(chunks):
        pool_copy[k].start()
    for k in range(chunks):
        docs_copy[k].start()

    owner_row = owner_ref[...]
    row_row = row_ref[...]
    down = lax.broadcasted_iota(jnp.int32, (share, share), 0)
    across = lax.broadcasted_iota(jnp.int32, (share, share), 1)
    wide = jnp.broadcast_to(owner_row, (share, share)).astype(jnp.float32)
    owner_col = jnp.sum(jnp.where(down == across, wide, 0.0), axis=1, keepdims=True)
    rank_row = jnp.sum(
        jnp.where((owner_col == wide) & (down < across), 1.0, 0.0), axis=0, keepdims=True
    )
    owner_f = owner_row.astype(jnp.float32)
    asked_row = owner_f * SUB + rank_row
    slot_row = owner_f * cap + rank_row
    slot_col = jnp.sum(
        jnp.where(down == across, jnp.broadcast_to(slot_row, (share, share)), 0.0),
        axis=1, keepdims=True,
    )
    place = lax.broadcasted_iota(jnp.int32, (slabs * SUB, share), 0).astype(jnp.float32)
    asked = jnp.sum(
        jnp.where(place == asked_row, row_row.astype(jnp.float32), 0.0), axis=1, keepdims=True
    )
    req_out[...] = jnp.broadcast_to(asked, (slabs * SUB, LANES)).astype(jnp.int32).reshape(
        slabs, SUB, LANES
    )
    choose = jnp.where(
        slot_col == lax.broadcasted_iota(jnp.int32, (share, slabs * cap), 1).astype(jnp.float32),
        1.0, 0.0,
    ).astype(jnp.bfloat16)

    pl.semaphore_wait(barrier, slabs + loops - 2)

    def req_copy(d):
        other = lax.rem(slab + d, slabs)
        return pltpu.make_async_remote_copy(
            src_ref=req_out.at[other], dst_ref=req_in.at[slab],
            send_sem=req_send.at[d], recv_sem=req_recv.at[d],
            device_id=(other, loop), device_id_type=MESH,
        )

    for d in range(1, slabs):
        req_copy(d).start()
    own_req = pltpu.make_async_copy(req_out.at[slab], req_in.at[slab], self_sem.at[chunks])
    own_req.start()
    own_req.wait()
    for d in range(1, slabs):
        req_copy(d).wait()

    wanted = req_in[...].reshape(slabs * SUB, LANES)
    lane = lax.broadcasted_iota(jnp.int32, (slabs * SUB, LANES), 1)
    pick = jnp.concatenate(
        [
            jnp.where(wanted == lane + b * LANES, 1.0, 0.0).astype(jnp.bfloat16)
            for b in range(rows_pool // LANES)
        ],
        axis=1,
    )

    def pick_copy(k, d):
        other = lax.rem(slab + d, slabs)
        return pltpu.make_async_remote_copy(
            src_ref=picked.at[k, other], dst_ref=fetched.at[k, slab],
            send_sem=pick_send.at[k, d], recv_sem=pick_recv.at[k, d],
            device_id=(other, loop), device_id_type=MESH,
        )

    def own_pick(k):
        return pltpu.make_async_copy(picked.at[k, slab], fetched.at[k, slab], self_sem.at[k])

    def gather(k):
        pool_copy[k].wait()
        rows = jnp.dot(
            pick, pool[:, k * chunk:(k + 1) * chunk], preferred_element_type=jnp.float32
        )
        for r in range(slabs):
            picked[k, r] = rows[r * SUB:r * SUB + cap].astype(jnp.bfloat16)
        for d in range(1, slabs):
            pick_copy(k, d).start()
        own_pick(k).start()

    def unit_of(j, pos, c):
        return (2 * j + c) * loops + loop_of(pos)

    def unit_copy(k, j, pos, way):
        u = unit_of(j, pos, core)
        device = ((slab, ahead), (slab, behind), (2 * line + 1 - core, loop))[way]
        return pltpu.make_async_remote_copy(
            src_ref=cand.at[k, u], dst_ref=cand.at[k, u],
            send_sem=unit_send.at[k, j * loops + pos, way], recv_sem=unit_recv.at[k, u],
            device_id=device, device_id_type=MESH,
        )

    def line_copy(k, d):
        return pltpu.make_async_remote_copy(
            src_ref=cand.at[k, me], dst_ref=cand.at[k, me],
            send_sem=line_send.at[k, d], recv_sem=unit_recv.at[k, me],
            device_id=(lax.rem(slab + 2 * d, slabs), loop), device_id_type=MESH,
        )

    def arrive(k, j, pos, c):
        u = unit_of(j, pos, c)
        pltpu.make_async_remote_copy(
            src_ref=cand.at[k, u], dst_ref=cand.at[k, u],
            send_sem=unit_send.at[k, 0, 0], recv_sem=unit_recv.at[k, u],
            device_id=(2 * line + 1 - core, loop), device_id_type=MESH,
        ).wait_recv()

    reach_even, reach_odd = half, loops - 1 - half

    def forward(k, j, pos, finish=False):
        def act(cond, way):
            @pl.when(cond)
            def _():
                copy = unit_copy(k, j, pos, way)
                if finish:
                    copy.wait_send()
                else:
                    copy.start()
        from_here = pos == here
        far_ahead = lax.rem(here - pos + loops, loops)
        far_behind = lax.rem(pos - here + loops, loops)
        reach_ahead = jnp.where(core == 0, reach_even, reach_odd)
        reach_behind = jnp.where(core == 0, reach_odd, reach_even)
        by_ahead = far_ahead <= reach_ahead
        act(from_here | (by_ahead & (far_ahead < reach_ahead)), 0)
        act(from_here | (jnp.logical_not(by_ahead) & (far_behind < reach_behind)), 1)
        act(from_here | True, 2)

    def nearby(first, action):
        def step(t, _):
            far = (t + 1) // 2
            j = jnp.where(lax.rem(t, 2) == 1, line - far, line + far)

            @pl.when((j >= 0) & (j < lines))
            def _():
                action(j)
            return 0
        lax.fori_loop(first, 2 * lines - 1, step, 0)

    def own(k):
        own_pick(k).wait()
        for d in range(1, slabs):
            pick_copy(k, d).wait()
        rows = jnp.concatenate(
            [fetched[k, o].astype(jnp.float32) for o in range(slabs)], axis=0
        ).astype(jnp.bfloat16)
        mine = jnp.dot(choose, rows, preferred_element_type=jnp.float32)
        cand[k, me] = mine.astype(jnp.bfloat16)
        forward(k, line, here)
        for d in range(1, lines):
            line_copy(k, d).start()

    def column(k):
        def action(j):
            arrive(k, j, here, core)
            forward(k, j, here)
        nearby(1, action)

    def ring(k, e):
        def action(j):
            behind_pos = lax.rem(here - e + loops, loops)
            ahead_pos = lax.rem(here + e, loops)
            reach_ahead = jnp.where(core == 0, reach_even, reach_odd)
            reach_behind = jnp.where(core == 0, reach_odd, reach_even)

            @pl.when(e <= reach_ahead)
            def _():
                arrive(k, j, behind_pos, core)
                forward(k, j, behind_pos)

            @pl.when(e <= reach_behind)
            def _():
                arrive(k, j, ahead_pos, core)
                forward(k, j, ahead_pos)
        nearby(0, action)

    def sibling(k):
        def step(t, _):
            arrive(k, t // loops, lax.rem(t, loops), 1 - core)
            return 0
        lax.fori_loop(0, lines * loops, step, 0)

    def multiply(k, piece):
        if piece == 0:
            docs_copy[k].wait()
        share_all = cand[k].reshape(units * share, chunk)
        rows = n_docs // pieces
        for i in range(rows // tile):
            at = pl.ds(piece * rows + i * tile, tile)
            product = lax.dot_general(
                docs[k, at, :], share_all, (((1,), (1,)), ((), ())),
                preferred_element_type=jnp.float32,
            )
            if k == 0:
                acc[at, :] = product
            else:
                acc[at, :] += product

    for k in range(chunks):
        gather(k)
    for k in range(min(2, chunks)):
        own(k)
    for t in range(chunks + half + 1):
        stages = []
        if 0 < t < chunks - 1:
            stages.append(functools.partial(own, t + 1))
        if t < chunks:
            stages.append(functools.partial(column, t))
        for e in range(1, half + 1):
            if 0 <= t - e < chunks:
                stages.append(functools.partial(ring, t - e, e))
        if 0 <= t - half < chunks:
            stages.append(functools.partial(sibling, t - half))
        done = t - half - 1
        for piece in range(max(pieces, len(stages))):
            if piece < len(stages):
                stages[piece]()
            if done >= 0 and piece < pieces:
                multiply(done, piece)

    cover_cols = jnp.transpose(cover_ref[...])
    weight_cols = jnp.transpose(weight_ref[...])
    total = jnp.zeros((1, units * share), jnp.float32)
    for j in range(n_docs // LANES):
        s = acc[j * LANES:(j + 1) * LANES, :] * scale
        gain = weight_cols[:, j:j + 1] * jnp.maximum(s - cover_cols[:, j:j + 1], 0.0)
        total = total + jnp.sum(gain, axis=0, keepdims=True)
    total = total / total_docs
    for r in range(units * share // LANES):
        part[r] = total[:, r * LANES:(r + 1) * LANES]
    per_row = LANES // (loops * share)

    def slab_term(d):
        other = lax.rem(slab + d, slabs)
        return pltpu.make_async_remote_copy(
            src_ref=part.at[other // per_row], dst_ref=slab_terms.at[d],
            send_sem=slab_send.at[d], recv_sem=slab_recv.at[d],
            device_id=(other, loop), device_id_type=MESH,
        )

    def loop_term(d):
        return pltpu.make_async_remote_copy(
            src_ref=loop_terms.at[0], dst_ref=loop_terms.at[d],
            send_sem=loop_send.at[d], recv_sem=loop_recv.at[d],
            device_id=(slab, lax.rem(loop + d, loops)), device_id_type=MESH,
        )

    for d in range(1, slabs):
        slab_term(d).start()
    slab_terms[0] = part[slab // per_row]
    for k in range(chunks):
        for d in range(1, lines):
            line_copy(k, d).wait_send()

        def finish(t, _, k=k):
            forward(k, t // loops, lax.rem(t, loops), finish=True)
            return 0
        lax.fori_loop(0, lines * loops, finish, 0)
    for d in range(1, slabs):
        slab_term(d).wait()
    loop_terms[0] = jnp.sum(slab_terms[...], axis=0)
    for d in range(1, loops):
        loop_term(d).start()
    for d in range(1, loops):
        loop_term(d).wait()
    out_ref[...] = jnp.sum(loop_terms[...], axis=0)


def body(dims, doc_pool, cand_owner, cand_row, elements, coverage, elem_weight):
    slabs, loops, share, cap, chunks, chunk, tile, _, _ = dims
    pool_rows, width = doc_pool.shape[2:]
    n_docs = elements.shape[2]
    units = slabs * loops
    per_row = LANES // share
    vmem = pl.BlockSpec(memory_space=pltpu.VMEM)
    hbm = pl.BlockSpec(memory_space=pl.ANY)
    dma = pltpu.SemaphoreType.DMA
    out = pl.pallas_call(
        functools.partial(kernel, dims),
        out_shape=jax.ShapeDtypeStruct((1, LANES), jnp.float32),
        in_specs=[vmem, vmem, vmem, vmem, hbm, hbm],
        out_specs=vmem,
        scratch_shapes=[
            pltpu.VMEM((pool_rows, width), jnp.bfloat16),
            pltpu.VMEM((chunks, n_docs, chunk), jnp.bfloat16),
            pltpu.VMEM((slabs, SUB, LANES), jnp.int32),
            pltpu.VMEM((slabs, SUB, LANES), jnp.int32),
            pltpu.VMEM((chunks, slabs, cap, chunk), jnp.bfloat16),
            pltpu.VMEM((chunks, slabs, cap, chunk), jnp.bfloat16),
            pltpu.VMEM((chunks, units, share, chunk), jnp.bfloat16),
            pltpu.VMEM((n_docs, units * share), jnp.float32),
            pltpu.VMEM((units * share // LANES, 1, LANES), jnp.float32),
            pltpu.VMEM((slabs, 1, LANES), jnp.float32),
            pltpu.VMEM((loops, 1, LANES), jnp.float32),
            dma((chunks,)),
            dma((chunks,)),
            dma((slabs,)),
            dma((slabs,)),
            dma((chunks, slabs)),
            dma((chunks, slabs)),
            dma((chunks + 1,)),
            dma((chunks, units // 2, 3)),
            dma((chunks, slabs // 2)),
            dma((chunks, units)),
            dma((slabs,)),
            dma((slabs,)),
            dma((loops,)),
            dma((loops,)),
        ],
        compiler_params=pltpu.CompilerParams(
            collective_id=0, has_side_effects=True, vmem_limit_bytes=60 * 2**20
        ),
    )(
        cand_owner.reshape(1, share),
        cand_row.reshape(1, share),
        coverage.reshape(n_docs // LANES, LANES),
        elem_weight.reshape(n_docs // LANES, LANES),
        doc_pool.reshape(pool_rows, width),
        elements.reshape(n_docs, width),
    )
    me = lax.axis_index("slab") * loops + lax.axis_index("loop")
    mine = lax.dynamic_slice(out, (0, lax.rem(me, per_row) * share), (1, share))
    return mine.reshape(1, 1, share)


def solution(mesh):
    slabs, loops = mesh.shape["slab"], mesh.shape["loop"]

    def whole(doc_pool, cand_owner, cand_row, elements, coverage, elem_weight):
        share = cand_row.shape[2]
        width = doc_pool.shape[3]
        n_docs = elements.shape[2]
        cap = max(2, 2 * share // slabs)
        chunks = 4
        dims = (
            slabs, loops, share, cap, chunks, width // chunks, min(1024, n_docs),
            float(n_docs * slabs * loops), float(width) ** (-0.5),
        )
        placed = (
            P("slab", "loop", None, None),
            P("slab", "loop", None, None),
            P("slab", "loop", None),
            P("slab", "loop", None, None),
            P("slab", "loop", None),
            P("slab", "loop", None),
        )
        return jax.shard_map(
            functools.partial(body, dims), mesh=mesh, in_specs=placed,
            out_specs=P("slab", "loop", None), check_vma=False,
        )(doc_pool, cand_owner, cand_row, elements, coverage, elem_weight)

    return whole
```

```python
import functools

import jax
import jax.numpy as jnp
from jax import lax
from jax.experimental import pallas as pl
from jax.experimental.pallas import tpu as pltpu
from jax.sharding import PartitionSpec as P

MESH = pl.DeviceIdType.MESH
LANES = 128
SUB = 8


def kernel(
    dims,
    owner_ref, row_ref, cover_ref, weight_ref, pool_hbm, docs_hbm,
    out_ref,
    pool, docs, req_out, req_in, picked, fetched, cand, acc, part, slab_terms,
    loop_terms,
    pool_sem, docs_sem, req_send, req_recv, pick_send, pick_recv, self_sem,
    unit_send, line_send, unit_recv, slab_send, slab_recv, loop_send, loop_recv,
):
    slabs, loops, share, cap, chunks, chunk, tile, total_docs, scale = dims
    lines = slabs // 2
    units = slabs * loops
    rows_pool = pool.shape[0]
    n_docs = docs.shape[1]
    slab = lax.axis_index("slab")
    loop = lax.axis_index("loop")
    line = slab // 2
    core = lax.rem(slab, 2)
    me = slab * loops + loop
    half = loops // 2
    pieces = 4

    def loop_of(pos):
        return jnp.where(pos < half, 2 * pos, 2 * (loops - 1 - pos) + 1)

    here = jnp.where(lax.rem(loop, 2) == 0, loop // 2, loops - 1 - loop // 2)
    ahead = loop_of(lax.rem(here + 1, loops))
    behind = loop_of(lax.rem(here + loops - 1, loops))

    pool_copy = [
        pltpu.make_async_copy(
            pool_hbm.at[:, pl.ds(k * chunk, chunk)],
            pool.at[:, pl.ds(k * chunk, chunk)],
            pool_sem.at[k],
        )
        for k in range(chunks)
    ]
    docs_copy = [
        pltpu.make_async_copy(
            docs_hbm.at[:, pl.ds(k * chunk, chunk)], docs.at[k], docs_sem.at[k]
        )
        for k in range(chunks)
    ]

    barrier = pltpu.get_barrier_semaphore()

    def greet(device):
        pl.semaphore_signal(barrier, inc=1, device_id=device, device_id_type=MESH)

    for d in range(1, slabs):
        greet((lax.rem(slab + d, slabs), loop))
    for d in range(1, loops):
        greet((slab, lax.rem(loop + d, loops)))
    for k in range(chunks):
        pool_copy[k].start()
    for k in range(chunks):
        docs_copy[k].start()

    owner_row = owner_ref[...]
    row_row = row_ref[...]
    down = lax.broadcasted_iota(jnp.int32, (share, share), 0)
    across = lax.broadcasted_iota(jnp.int32, (share, share), 1)
    wide = jnp.broadcast_to(owner_row, (share, share)).astype(jnp.float32)
    owner_col = jnp.sum(jnp.where(down == across, wide, 0.0), axis=1, keepdims=True)
    rank_row = jnp.sum(
        jnp.where((owner_col == wide) & (down < across), 1.0, 0.0), axis=0, keepdims=True
    )
    owner_f = owner_row.astype(jnp.float32)
    asked_row = owner_f * SUB + rank_row
    slot_row = owner_f * cap + rank_row
    slot_col = jnp.sum(
        jnp.where(down == across, jnp.broadcast_to(slot_row, (share, share)), 0.0),
        axis=1, keepdims=True,
    )
    place = lax.broadcasted_iota(jnp.int32, (slabs * SUB, share), 0).astype(jnp.float32)
    asked = jnp.sum(
        jnp.where(place == asked_row, row_row.astype(jnp.float32), 0.0), axis=1, keepdims=True
    )
    req_out[...] = jnp.broadcast_to(asked, (slabs * SUB, LANES)).astype(jnp.int32).reshape(
        slabs, SUB, LANES
    )
    choose = jnp.where(
        slot_col == lax.broadcasted_iota(jnp.int32, (share, slabs * cap), 1).astype(jnp.float32),
        1.0, 0.0,
    ).astype(jnp.bfloat16)

    pl.semaphore_wait(barrier, slabs + loops - 2)

    def req_copy(d):
        other = lax.rem(slab + d, slabs)
        return pltpu.make_async_remote_copy(
            src_ref=req_out.at[other], dst_ref=req_in.at[slab],
            send_sem=req_send.at[d], recv_sem=req_recv.at[d],
            device_id=(other, loop), device_id_type=MESH,
        )

    for d in range(1, slabs):
        req_copy(d).start()
    own_req = pltpu.make_async_copy(req_out.at[slab], req_in.at[slab], self_sem.at[chunks])
    own_req.start()
    own_req.wait()
    for d in range(1, slabs):
        req_copy(d).wait()

    wanted = req_in[...].reshape(slabs * SUB, LANES)
    lane = lax.broadcasted_iota(jnp.int32, (slabs * SUB, LANES), 1)
    pick = jnp.concatenate(
        [
            jnp.where(wanted == lane + b * LANES, 1.0, 0.0).astype(jnp.bfloat16)
            for b in range(rows_pool // LANES)
        ],
        axis=1,
    )

    def pick_copy(k, d):
        other = lax.rem(slab + d, slabs)
        return pltpu.make_async_remote_copy(
            src_ref=picked.at[k, other], dst_ref=fetched.at[k, slab],
            send_sem=pick_send.at[k, d], recv_sem=pick_recv.at[k, d],
            device_id=(other, loop), device_id_type=MESH,
        )

    def own_pick(k):
        return pltpu.make_async_copy(picked.at[k, slab], fetched.at[k, slab], self_sem.at[k])

    def gather(k):
        pool_copy[k].wait()
        rows = jnp.dot(
            pick, pool[:, k * chunk:(k + 1) * chunk], preferred_element_type=jnp.float32
        )
        for r in range(slabs):
            picked[k, r] = rows[r * SUB:r * SUB + cap].astype(jnp.bfloat16)
        for d in range(1, slabs):
            pick_copy(k, d).start()
        own_pick(k).start()

    def unit_of(j, pos, c):
        return (2 * j + c) * loops + loop_of(pos)

    def unit_copy(k, j, pos, way):
        u = unit_of(j, pos, core)
        device = ((slab, ahead), (slab, behind), (2 * line + 1 - core, loop))[way]
        return pltpu.make_async_remote_copy(
            src_ref=cand.at[k, u], dst_ref=cand.at[k, u],
            send_sem=unit_send.at[k, j * loops + pos, way], recv_sem=unit_recv.at[k, u],
            device_id=device, device_id_type=MESH,
        )

    def line_copy(k, d):
        return pltpu.make_async_remote_copy(
            src_ref=cand.at[k, me], dst_ref=cand.at[k, me],
            send_sem=line_send.at[k, d], recv_sem=unit_recv.at[k, me],
            device_id=(lax.rem(slab + 2 * d, slabs), loop), device_id_type=MESH,
        )

    def arrive(k, j, pos, c):
        u = unit_of(j, pos, c)
        pltpu.make_async_remote_copy(
            src_ref=cand.at[k, u], dst_ref=cand.at[k, u],
            send_sem=unit_send.at[k, 0, 0], recv_sem=unit_recv.at[k, u],
            device_id=(2 * line + 1 - core, loop), device_id_type=MESH,
        ).wait_recv()

    reach_even, reach_odd = half, loops - 1 - half

    def forward(k, j, pos, finish=False):
        def act(cond, way):
            @pl.when(cond)
            def _():
                copy = unit_copy(k, j, pos, way)
                if finish:
                    copy.wait_send()
                else:
                    copy.start()
        from_here = pos == here
        far_ahead = lax.rem(here - pos + loops, loops)
        far_behind = lax.rem(pos - here + loops, loops)
        reach_ahead = jnp.where(core == 0, reach_even, reach_odd)
        reach_behind = jnp.where(core == 0, reach_odd, reach_even)
        by_ahead = far_ahead <= reach_ahead
        act(from_here | (by_ahead & (far_ahead < reach_ahead)), 0)
        act(from_here | (jnp.logical_not(by_ahead) & (far_behind < reach_behind)), 1)
        act(from_here | True, 2)

    def nearby(first, action):
        def step(t, _):
            far = (t + 1) // 2
            j = jnp.where(lax.rem(t, 2) == 1, line - far, line + far)

            @pl.when((j >= 0) & (j < lines))
            def _():
                action(j)
            return 0
        lax.fori_loop(first, 2 * lines - 1, step, 0)

    def own(k):
        own_pick(k).wait()
        for d in range(1, slabs):
            pick_copy(k, d).wait()
        rows = jnp.concatenate(
            [fetched[k, o].astype(jnp.float32) for o in range(slabs)], axis=0
        ).astype(jnp.bfloat16)
        mine = jnp.dot(choose, rows, preferred_element_type=jnp.float32)
        cand[k, me] = mine.astype(jnp.bfloat16)
        forward(k, line, here)
        for d in range(1, lines):
            line_copy(k, d).start()

    def column(k):
        def action(j):
            arrive(k, j, here, core)
            forward(k, j, here)
        nearby(1, action)

    def ring(k, e):
        def action(j):
            behind_pos = lax.rem(here - e + loops, loops)
            ahead_pos = lax.rem(here + e, loops)
            reach_ahead = jnp.where(core == 0, reach_even, reach_odd)
            reach_behind = jnp.where(core == 0, reach_odd, reach_even)

            @pl.when(e <= reach_ahead)
            def _():
                arrive(k, j, behind_pos, core)
                forward(k, j, behind_pos)

            @pl.when(e <= reach_behind)
            def _():
                arrive(k, j, ahead_pos, core)
                forward(k, j, ahead_pos)
        nearby(0, action)

    def sibling(k):
        def step(t, _):
            arrive(k, t // loops, lax.rem(t, loops), 1 - core)
            return 0
        lax.fori_loop(0, lines * loops, step, 0)

    def multiply(k, piece):
        if piece == 0:
            docs_copy[k].wait()
        share_all = cand[k].reshape(units * share, chunk)
        rows = n_docs // pieces
        for i in range(rows // tile):
            at = pl.ds(piece * rows + i * tile, tile)
            product = lax.dot_general(
                docs[k, at, :], share_all, (((1,), (1,)), ((), ())),
                preferred_element_type=jnp.float32,
            )
            if k == 0:
                acc[at, :] = product
            else:
                acc[at, :] += product

    for k in range(chunks):
        gather(k)
    for k in range(min(2, chunks)):
        own(k)
    for t in range(chunks + half + 1):
        stages = []
        if 0 < t < chunks - 1:
            stages.append(functools.partial(own, t + 1))
        if t < chunks:
            stages.append(functools.partial(column, t))
        for e in range(1, half + 1):
            if 0 <= t - e < chunks:
                stages.append(functools.partial(ring, t - e, e))
        if 0 <= t - half < chunks:
            stages.append(functools.partial(sibling, t - half))
        done = t - half - 1
        for piece in range(max(pieces, len(stages))):
            if piece < len(stages):
                stages[piece]()
            if done >= 0 and piece < pieces:
                multiply(done, piece)

    cover_cols = jnp.transpose(cover_ref[...])
    weight_cols = jnp.transpose(weight_ref[...])
    total = jnp.zeros((1, units * share), jnp.float32)
    for j in range(n_docs // LANES):
        s = acc[j * LANES:(j + 1) * LANES, :] * scale
        gain = weight_cols[:, j:j + 1] * jnp.maximum(s - cover_cols[:, j:j + 1], 0.0)
        total = total + jnp.sum(gain, axis=0, keepdims=True)
    total = total / total_docs
    for r in range(units * share // LANES):
        part[r] = total[:, r * LANES:(r + 1) * LANES]
    per_row = LANES // (loops * share)

    def slab_term(d):
        other = lax.rem(slab + d, slabs)
        return pltpu.make_async_remote_copy(
            src_ref=part.at[other // per_row], dst_ref=slab_terms.at[d],
            send_sem=slab_send.at[d], recv_sem=slab_recv.at[d],
            device_id=(other, loop), device_id_type=MESH,
        )

    def loop_term(d):
        return pltpu.make_async_remote_copy(
            src_ref=loop_terms.at[0], dst_ref=loop_terms.at[d],
            send_sem=loop_send.at[d], recv_sem=loop_recv.at[d],
            device_id=(slab, lax.rem(loop + d, loops)), device_id_type=MESH,
        )

    for d in range(1, slabs):
        slab_term(d).start()
    slab_terms[0] = part[slab // per_row]
    for k in range(chunks):
        for d in range(1, lines):
            line_copy(k, d).wait_send()

        def finish(t, _, k=k):
            forward(k, t // loops, lax.rem(t, loops), finish=True)
            return 0
        lax.fori_loop(0, lines * loops, finish, 0)
    for d in range(1, slabs):
        slab_term(d).wait()
    loop_terms[0] = jnp.sum(slab_terms[...], axis=0)
    for d in range(1, loops):
        loop_term(d).start()
    for d in range(1, loops):
        loop_term(d).wait()
    row = jnp.sum(loop_terms[...], axis=0)
    first = lax.rem(slab, per_row) * loops * share + loop * share
    mine = lax.broadcasted_iota(jnp.int32, (LANES, LANES), 0)
    to = lax.broadcasted_iota(jnp.int32, (LANES, LANES), 1)
    column_of = jnp.sum(
        jnp.where(mine == to, jnp.broadcast_to(row, (LANES, LANES)), 0.0), axis=1, keepdims=True
    )
    moved = jnp.sum(jnp.where(mine == to + first, column_of, 0.0), axis=0, keepdims=True)
    out_ref[...] = moved[:, :share]


def body(dims, doc_pool, cand_owner, cand_row, elements, coverage, elem_weight):
    slabs, loops, share, cap, chunks, chunk, tile, _, _ = dims
    pool_rows, width = doc_pool.shape[2:]
    n_docs = elements.shape[2]
    units = slabs * loops
    vmem = pl.BlockSpec(memory_space=pltpu.VMEM)
    hbm = pl.BlockSpec(memory_space=pl.ANY)
    dma = pltpu.SemaphoreType.DMA
    out = pl.pallas_call(
        functools.partial(kernel, dims),
        out_shape=jax.ShapeDtypeStruct((1, share), jnp.float32),
        in_specs=[vmem, vmem, vmem, vmem, hbm, hbm],
        out_specs=vmem,
        scratch_shapes=[
            pltpu.VMEM((pool_rows, width), jnp.bfloat16),
            pltpu.VMEM((chunks, n_docs, chunk), jnp.bfloat16),
            pltpu.VMEM((slabs, SUB, LANES), jnp.int32),
            pltpu.VMEM((slabs, SUB, LANES), jnp.int32),
            pltpu.VMEM((chunks, slabs, cap, chunk), jnp.bfloat16),
            pltpu.VMEM((chunks, slabs, cap, chunk), jnp.bfloat16),
            pltpu.VMEM((chunks, units, share, chunk), jnp.bfloat16),
            pltpu.VMEM((n_docs, units * share), jnp.float32),
            pltpu.VMEM((units * share // LANES, 1, LANES), jnp.float32),
            pltpu.VMEM((slabs, 1, LANES), jnp.float32),
            pltpu.VMEM((loops, 1, LANES), jnp.float32),
            dma((chunks,)),
            dma((chunks,)),
            dma((slabs,)),
            dma((slabs,)),
            dma((chunks, slabs)),
            dma((chunks, slabs)),
            dma((chunks + 1,)),
            dma((chunks, units // 2, 3)),
            dma((chunks, slabs // 2)),
            dma((chunks, units)),
            dma((slabs,)),
            dma((slabs,)),
            dma((loops,)),
            dma((loops,)),
        ],
        compiler_params=pltpu.CompilerParams(
            collective_id=0, has_side_effects=True, vmem_limit_bytes=60 * 2**20
        ),
    )(
        cand_owner.reshape(1, share),
        cand_row.reshape(1, share),
        coverage.reshape(n_docs // LANES, LANES),
        elem_weight.reshape(n_docs // LANES, LANES),
        doc_pool.reshape(pool_rows, width),
        elements.reshape(n_docs, width),
    )
    return out.reshape(1, 1, share)


def solution(mesh):
    slabs, loops = mesh.shape["slab"], mesh.shape["loop"]

    def whole(doc_pool, cand_owner, cand_row, elements, coverage, elem_weight):
        share = cand_row.shape[2]
        width = doc_pool.shape[3]
        n_docs = elements.shape[2]
        cap = max(2, 2 * share // slabs)
        chunks = 4
        dims = (
            slabs, loops, share, cap, chunks, width // chunks, min(512, n_docs),
            float(n_docs * slabs * loops), float(width) ** (-0.5),
        )
        placed = (
            P("slab", "loop", None, None),
            P("slab", "loop", None, None),
            P("slab", "loop", None),
            P("slab", "loop", None, None),
            P("slab", "loop", None),
            P("slab", "loop", None),
        )
        return jax.shard_map(
            functools.partial(body, dims), mesh=mesh, in_specs=placed,
            out_specs=P("slab", "loop", None), check_vma=False,
        )(doc_pool, cand_owner, cand_row, elements, coverage, elem_weight)

    return whole
```
